256 devices in a mesh: seq: 64 (over y, z, core), head: 4 (over x).
Axes of the slice: x: 4, y: 4, z: 8, core: 2. Of those that a mesh axis runs over, the one named last changes fastest.
Arguments:
- inner_input: bfloat16 [16384, 8192], P('seq', 'head'), may hold values from -6 to 6
- state_input: bfloat16 [16384, 2, 1024], P('seq', None, 'head'), may hold values from -3 to 3
- gate_input: bfloat16 [16384, 8192], P('seq', 'head'), may hold values from -6 to 6
- step_input: float32 [128, 16384], P('head', 'seq'), may hold values from -4.7 to 0.6
- decay_exponent: float32 [128], P('head')
- skip_gain: float32 [128], P('head'), may hold values from 0.5 to 1.5
- documents: int32 [16384], P('seq'), may hold values from 0 to 15, never falling along the last dimension, each value on 1 to 1536 neighbouring positions
- filter_inner: float32 [4, 8192], P(None, 'head'), may hold values from -3 to 3
- filter_state: float32 [4, 2, 1024], P(None, None, 'head'), may hold values from -3 to 3
- norm_gain: float32 [8192], P('head'), may hold values from 0.1 to 1.9
- output_weight: bfloat16 [8192, 4096], P('head', 'seq'), may hold values from -0.0625 to 0.0625
Outputs:
- mixed: bfloat16 [16384, 4096], P('seq', 'head')
The draws below stay inside these ranges and needn't reach their ends.
Inputs may be any that keep to these rules, and one draw needn't show every extreme that they name: `documents`: document numbers never fall along the sequence.
All inputs are finite; a program needn't handle non-finite values.
Results may differ from the reference program's by a relative error of at most 0.0058.
Values may be sent and summed in bfloat16 or wider, within the bound.
No kernel may reach another device: no remote copies, remote signals or barrier semaphores. Data moves between devices by JAX's collectives and lax.ppermute only.
A program may use at most 192 MiB of HBM per device.

```python
import math
import jax
import jax.numpy as jnp
import numpy as np
from jax import lax

D = 4096
HEADS = 128
HEAD_DIM = 64
STATE = 128
GROUPS = 8
INNER = 8192
KERNEL = 4
SPAN = 256
TOK_DEV = 256
TOKENS = 16384
DOCS = 16
DOC_MOST = 1536


def head_split(key):
    chosen = jax.random.uniform(jax.random.fold_in(key, 101), (HEADS,))
    share = 0.5
    return chosen < share


def draw_step_input(key, part):
    slow = head_split(key)
    base_step = jnp.where(slow, 0.02, 0.5)
    roughness = jnp.exp(jax.random.uniform(jax.random.fold_in(key, 202), (HEADS, TOKENS), minval=-0.7, maxval=0.7))
    value = base_step[:, None] * roughness
    return jnp.log(jnp.expm1(value)).astype(jnp.float32)


def draw_decay_exponent(key, part):
    slow = head_split(key)
    position = jax.random.uniform(jax.random.fold_in(key, 303), (HEADS,))
    slow_rate = 0.3 * jnp.power(5.0, position) / (6.0 * TOK_DEV)
    fast_rate = 0.02 * jnp.power(2.0, position)
    base_step = jnp.where(slow, 0.02, 0.5)
    chosen_rate = jnp.where(slow, slow_rate, fast_rate)
    return jnp.log(chosen_rate / base_step).astype(jnp.float32)


def level_of(key, dims, shards, low, high):
    def one(dim, shards_of):
        steps = jax.random.uniform(jax.random.fold_in(jax.random.fold_in(key, 6), dim), (shards_of,), jnp.float32, low / len(shards), high / len(shards))
        return jnp.repeat(jnp.exp(steps), dims[dim] // shards_of).reshape((-1,) + (1,) * (len(dims) - dim - 1))

    level = one(*shards[0])
    for cut in shards[1:]:
        level = level * one(*cut)
    return level


def split_up(count, total, most, lean):
    portions = [(1 << 20) // math.isqrt(rank ** lean) + 1 for rank in range(2, count + 1)]
    surplus, holding = total - most - (count - 1), [1] * (count - 1)
    while surplus > 0:
        movable = [i for i in range(count - 1) if holding[i] < most]
        whole, remaining = sum([portions[i] for i in movable]), surplus
        for i in movable:
            addition = min(most - holding[i], max(1, remaining * portions[i] // whole), surplus)
            holding[i] = holding[i] + addition
            surplus = surplus - addition
    return np.array([most] + holding)


def ragged(stream_key, amount, total, limit, lean):
    if amount == 2:
        one = jax.random.randint(stream_key, (), max(1, total - limit), min(limit, total - 1) + 1)
        return jnp.stack([one, total - one])
    lengths = jnp.asarray(split_up(amount, total, limit, lean), jnp.int32)
    couples = (amount - 1) // 2
    source_of, receiver = lengths[1:1 + 2 * couples:2], lengths[2:2 + 2 * couples:2]
    room = jnp.minimum(source_of - 1, limit - receiver)
    shifted = jax.random.randint(jax.random.fold_in(stream_key, 1), (couples,), 0, 1 << 20) % (room + 1)
    lengths = lengths.at[1:1 + 2 * couples:2].set(source_of - shifted).at[2:2 + 2 * couples:2].set(receiver + shifted)
    return lengths[jax.random.permutation(jax.random.fold_in(stream_key, 2), amount)]


def bell_draw(rng, extent, scale, most, cuts=(), dtype=jnp.bfloat16):
    values = jax.random.normal(rng, extent, jnp.float32) * scale
    if len(cuts) > 0:
        values = level_of(rng, extent, cuts, -0.22, 0.18) * values
    return jnp.clip(values, min=-most, max=most).astype(dtype)


def setup_inputs(seed: int = 0) -> dict:
    streams_of = jax.random.split(jax.random.key(seed), 12)
    return {
        "inner_input": bell_draw(streams_of[0], (TOKENS, INNER), 1.0, 6.0, ((0, 64), (1, 4))),
        "state_input": bell_draw(streams_of[1], (TOKENS, 2, GROUPS * STATE), 0.5, 3.0, ((0, 64), (2, 4))),
        "gate_input": bell_draw(streams_of[2], (TOKENS, INNER), 1.0, 6.0, ((0, 64), (1, 4))),
        "step_input": draw_step_input(jax.random.fold_in(streams_of[11], 71), 0),
        "decay_exponent": draw_decay_exponent(jax.random.fold_in(streams_of[11], 71), 0),
        "skip_gain": jnp.clip(0.5 + 1.0 * jax.random.uniform(streams_of[5], (HEADS,), jnp.float32) ** level_of(streams_of[5], (HEADS,), ((0, 4),), -0.2, 0.2), 0.5, 1.5),
        "documents": jnp.searchsorted(jnp.cumsum(ragged(streams_of[6], DOCS, TOKENS, DOC_MOST, 1)), jnp.arange(TOKENS), side="right").astype(jnp.int32),
        "filter_inner": bell_draw(streams_of[7], (KERNEL, INNER), KERNEL ** -0.5, 3.0, ((1, 4),), jnp.float32),
        "filter_state": bell_draw(streams_of[8], (KERNEL, 2, GROUPS * STATE), KERNEL ** -0.5, 3.0, ((2, 4),), jnp.float32),
        "norm_gain": jnp.clip(1.0 + 0.18 * jax.random.normal(streams_of[9], (INNER,), jnp.float32), 0.1, 1.9),
        "output_weight": bell_draw(streams_of[10], (INNER, D), INNER ** -0.5, 0.0625, ((0, 4), (1, 64))),
    }


highest = lax.Precision.HIGHEST

def causal_conv(extended, weights, segments_wide, segment_block):
    length = segment_block.shape[0]
    running = jnp.zeros(extended[:length].shape, jnp.float32)
    for offset in range(KERNEL):
        window = extended[offset:offset + length].astype(jnp.float32)
        matches = segments_wide[offset:offset + length] == segment_block
        matches = matches.reshape((length,) + (1,) * (extended.ndim - 1))
        running = running + jnp.where(matches, window * weights[offset], jnp.float32(0.0))
    return jax.nn.silu(running).astype(jnp.bfloat16)

def span_parts(values, write_rows, read_rows, step_size, decay_rate, segment_block, prior_segment):
    length = segment_block.shape[0]
    repeat = decay_rate.shape[0] // write_rows.shape[1]
    cumulative = jnp.cumsum(decay_rate, axis=1)
    places = jnp.arange(length)
    linked = (segment_block[:, None] == segment_block[None, :]) & (places[:, None] >= places[None, :])
    spread = cumulative[:, :, None] - cumulative[:, None, :]
    decays = jnp.exp(jnp.where(linked[None], spread, -jnp.inf))
    scores = jnp.einsum('ign,jgn->gij', read_rows.astype(jnp.float32), write_rows.astype(jnp.float32), precision=highest)
    scores = jnp.repeat(scores, repeat, axis=0)
    mixing = lax.optimization_barrier((decays * scores * step_size[:, None, :]).astype(jnp.bfloat16))
    within = jnp.einsum('hij,jhp->ihp', mixing.astype(jnp.float32), values.astype(jnp.float32), precision=highest)
    inflow = jnp.exp(cumulative) * (segment_block == prior_segment)[None, :].astype(jnp.float32)
    final_segment = segment_block[-1]
    closing = jnp.exp(cumulative[:, -1:] - cumulative) * (segment_block == final_segment)[None, :].astype(jnp.float32) * step_size
    weighted = lax.optimization_barrier((values.astype(jnp.float32) * closing.T[:, :, None]).astype(jnp.bfloat16))
    writes = jnp.repeat(write_rows, repeat, axis=1).astype(jnp.float32)
    deposit = jnp.einsum('jhp,jhn->hpn', weighted.astype(jnp.float32), writes, precision=highest)
    fading = jnp.exp(cumulative[:, -1]) * (final_segment == prior_segment).astype(jnp.float32)
    return (within, inflow, fading, deposit)

def reading(read_rows, held_state, repeat):
    readers = jnp.repeat(read_rows, repeat, axis=1).astype(jnp.float32)
    return jnp.einsum('ihn,hpn->ihp', readers, held_state, precision=highest)

def gated_norm(outputs, gates, norm_scale):
    height = outputs.shape[0]
    gated = outputs * jax.nn.silu(gates.astype(jnp.float32))
    grouped = gated.reshape(height, -1, INNER // GROUPS)
    mean_square = lax.optimization_barrier(jnp.mean(grouped * grouped, axis=-1, keepdims=True))
    normed = (grouped * lax.rsqrt(mean_square + 1e-05)).reshape(height, -1) * norm_scale
    return normed.astype(jnp.bfloat16)

def reference(inner_input, state_input, gate_input, step_input, decay_exponent, skip_gain, documents, filter_inner, filter_state, norm_gain, output_weight):
    span_count = TOKENS // SPAN
    margin = KERNEL - 1
    repeat = HEADS // GROUPS
    inner_blocks = inner_input.reshape(span_count, SPAN, INNER)
    state_blocks = state_input.reshape(span_count, SPAN, 2, GROUPS * STATE)
    gate_blocks = gate_input.reshape(span_count, SPAN, INNER)
    raw_blocks = step_input.reshape(HEADS, span_count, SPAN).transpose(1, 0, 2)
    segment_blocks = documents.reshape(span_count, SPAN)

    def advance(carried, pieces):
        state_now, prior_inner, prior_state, prior_segments = carried
        inner_block, state_block, gate_block, raw_block, segment_block = pieces
        segments_wide = jnp.concatenate([prior_segments, segment_block])
        inner_conv = causal_conv(jnp.concatenate([prior_inner, inner_block]), filter_inner, segments_wide, segment_block)
        state_conv = causal_conv(jnp.concatenate([prior_state, state_block]), filter_state, segments_wide, segment_block)
        values = inner_conv.reshape(SPAN, HEADS, HEAD_DIM)
        write_rows = state_conv[:, 0].reshape(SPAN, GROUPS, STATE)
        read_rows = state_conv[:, 1].reshape(SPAN, GROUPS, STATE)
        step_size = jax.nn.softplus(raw_block)
        decay_rate = -step_size * jnp.exp(decay_exponent)[:, None]
        within, inflow, fading, deposit = span_parts(values, write_rows, read_rows, step_size, decay_rate, segment_block, prior_segments[-1])
        scan_out = within + inflow.T[:, :, None] * reading(read_rows, state_now, repeat) + skip_gain[None, :, None] * values.astype(jnp.float32)
        state_now = fading[:, None, None] * state_now + deposit
        normed = gated_norm(scan_out.reshape(SPAN, INNER), gate_block, norm_gain)
        mixed = jnp.dot(normed, output_weight, preferred_element_type=jnp.float32).astype(jnp.bfloat16)
        return ((state_now, inner_block[-margin:], state_block[-margin:], segment_block[-margin:]), mixed)
    initial = (jnp.zeros((HEADS, HEAD_DIM, STATE), jnp.float32), jnp.zeros((margin, INNER), jnp.bfloat16), jnp.zeros((margin, 2, GROUPS * STATE), jnp.bfloat16), jnp.full((margin,), -1, jnp.int32))
    _, mixed = lax.scan(advance, initial, (inner_blocks, state_blocks, gate_blocks, raw_blocks, segment_blocks))
    return mixed.reshape(TOKENS, D)
```

```python
import jax
import jax.numpy as jnp
from jax import lax
from jax.sharding import PartitionSpec as P

HEAD_DIM = 64
STATE = 128
GROUPS = 8
INNER = 8192
KERNEL = 4
SPAN = 256
DOC_MOST = 1536
REACH = -(-(DOC_MOST - 1) // SPAN)


highest = lax.Precision.HIGHEST


def passed_along(value, axis, steps):
    count = lax.axis_size(axis)
    initial, last = (max(0, -steps), min(count, count - steps))
    return lax.ppermute(value, axis, [(source, source + steps) for source in range(initial, last)])


def causal_conv(extended, weights, segments_wide, segment_block):
    length = segment_block.shape[0]
    running = jnp.zeros(extended[:length].shape, jnp.float32)
    for offset in range(KERNEL):
        window = extended[offset : offset + length].astype(jnp.float32)
        matches = segments_wide[offset : offset + length] == segment_block
        matches = matches.reshape((length,) + (1,) * (extended.ndim - 1))
        running = running + jnp.where(matches, window * weights[offset], jnp.float32(0.0))
    return jax.nn.silu(running).astype(jnp.bfloat16)


def span_parts(values, write_rows, read_rows, step_size, decay_rate, segment_block, prior_segment):
    length = segment_block.shape[0]
    repeat = decay_rate.shape[0] // write_rows.shape[1]
    cumulative = jnp.cumsum(decay_rate, axis=1)
    places = jnp.arange(length)
    linked = (segment_block[:, None] == segment_block[None, :]) & (
        places[:, None] >= places[None, :]
    )
    spread = cumulative[:, :, None] - cumulative[:, None, :]
    decays = jnp.exp(jnp.where(linked[None], spread, -jnp.inf))
    scores = jnp.einsum("ign,jgn->gij", read_rows, write_rows, preferred_element_type=jnp.float32)
    scores = jnp.repeat(scores, repeat, axis=0)
    mixing = (decays * scores * step_size[:, None, :]).astype(jnp.bfloat16)
    within = jnp.einsum("hij,jhp->ihp", mixing, values, preferred_element_type=jnp.float32)
    inflow = jnp.exp(cumulative) * (segment_block == prior_segment)[None, :].astype(jnp.float32)
    final_segment = segment_block[-1]
    closing = (
        jnp.exp(cumulative[:, -1:] - cumulative)
        * (segment_block == final_segment)[None, :].astype(jnp.float32)
        * step_size
    )
    weighted = (values.astype(jnp.float32) * closing.T[:, :, None]).astype(jnp.bfloat16)
    writes = jnp.repeat(write_rows, repeat, axis=1)
    deposit = jnp.einsum("jhp,jhn->hpn", weighted, writes, preferred_element_type=jnp.float32)
    fading = jnp.exp(cumulative[:, -1]) * (final_segment == prior_segment).astype(jnp.float32)
    return (within, inflow, fading, deposit)


def reading(read_rows, held_state, repeat):
    readers = jnp.repeat(read_rows, repeat, axis=1).astype(jnp.float32)
    return jnp.einsum("ihn,hpn->ihp", readers, held_state, precision=highest)


def gated_norm(outputs, gates, norm_scale):
    height = outputs.shape[0]
    gated = outputs * jax.nn.silu(gates.astype(jnp.float32))
    grouped = gated.reshape(height, -1, INNER // GROUPS)
    mean_square = jnp.mean(grouped * grouped, axis=-1, keepdims=True)
    normed = (grouped * lax.rsqrt(mean_square + 1e-05)).reshape(height, -1) * norm_scale
    return normed.astype(jnp.bfloat16)


def chain_states(fading, deposit):
    carried = passed_along(deposit.astype(jnp.bfloat16), "seq", 1)
    for _ in range(REACH - 1):
        held = fading[:, None, None] * carried.astype(jnp.float32) + deposit
        carried = passed_along(held.astype(jnp.bfloat16), "seq", 1)
    return carried.astype(jnp.float32)


def on_device(
    inner_input,
    state_input,
    gate_input,
    step_input,
    decay_exponent,
    skip_gain,
    documents,
    filter_inner,
    filter_state,
    norm_gain,
    output_weight,
):
    weight = lax.all_gather(output_weight, "seq", axis=1, tiled=True)
    margin = KERNEL - 1
    length = documents.shape[0]
    head_count = decay_exponent.shape[0]
    groups = state_input.shape[2] // STATE
    repeat = head_count // groups
    before_inner, before_state, before_segments = passed_along(
        (inner_input[-margin:], state_input[-margin:], documents[-margin:].astype(jnp.bfloat16)),
        "seq",
        1,
    )
    segments_wide = jnp.concatenate([before_segments.astype(jnp.int32), documents])
    inner_conv = causal_conv(
        jnp.concatenate([before_inner, inner_input]), filter_inner, segments_wide, documents
    )
    state_conv = causal_conv(
        jnp.concatenate([before_state, state_input]), filter_state, segments_wide, documents
    )
    values = inner_conv.reshape(length, head_count, HEAD_DIM)
    write_rows = state_conv[:, 0].reshape(length, groups, STATE)
    read_rows = state_conv[:, 1].reshape(length, groups, STATE)
    step_size = jax.nn.softplus(step_input)
    decay_rate = -step_size * jnp.exp(decay_exponent)[:, None]
    skipped = skip_gain[None, :, None] * values.astype(jnp.float32)
    prior_segment = segments_wide[margin - 1]
    within, inflow, fading, deposit = span_parts(
        values, write_rows, read_rows, step_size, decay_rate, documents, prior_segment
    )
    carried = chain_states(fading, deposit)
    outputs = within + inflow.T[:, :, None] * reading(read_rows, carried, repeat) + skipped
    scan_out = outputs.reshape(length, head_count * HEAD_DIM)
    normed = gated_norm(scan_out, gate_input, norm_gain)
    partial_value = jnp.dot(normed, weight, preferred_element_type=jnp.float32)
    return lax.psum_scatter(
        partial_value.astype(jnp.bfloat16), "head", scatter_dimension=1, tiled=True
    )


def solution(mesh):
    placed = (
        P("seq", "head"),
        P("seq", None, "head"),
        P("seq", "head"),
        P("head", "seq"),
        P("head"),
        P("head"),
        P("seq"),
        P(None, "head"),
        P(None, None, "head"),
        P("head"),
        P("head", "seq"),
    )
    return jax.shard_map(
        on_device, mesh=mesh, in_specs=placed, out_specs=P("seq", "head"), check_vma=False
    )
```

```python
import jax
import jax.numpy as jnp
from jax import lax
from jax.sharding import PartitionSpec as P

HEAD_DIM = 64
STATE = 128
GROUPS = 8
INNER = 8192
KERNEL = 4
SPAN = 256
DOC_MOST = 1536
REACH = -(-(DOC_MOST - 1) // SPAN)


highest = lax.Precision.HIGHEST


def passed_along(value, axis, steps):
    count = lax.axis_size(axis)
    initial, last = (max(0, -steps), min(count, count - steps))
    return lax.ppermute(value, axis, [(source, source + steps) for source in range(initial, last)])


def causal_conv(extended, weights, segments_wide, segment_block):
    length = segment_block.shape[0]
    running = jnp.zeros(extended[:length].shape, jnp.float32)
    for offset in range(KERNEL):
        window = extended[offset : offset + length].astype(jnp.float32)
        matches = segments_wide[offset : offset + length] == segment_block
        matches = matches.reshape((length,) + (1,) * (extended.ndim - 1))
        running = running + jnp.where(matches, window * weights[offset], jnp.float32(0.0))
    return jax.nn.silu(running).astype(jnp.bfloat16)


def span_parts(values, write_rows, read_rows, step_size, decay_rate, segment_block, prior_segment):
    length = segment_block.shape[0]
    repeat = decay_rate.shape[0] // write_rows.shape[1]
    cumulative = jnp.cumsum(decay_rate, axis=1)
    places = jnp.arange(length)
    linked = (segment_block[:, None] == segment_block[None, :]) & (
        places[:, None] >= places[None, :]
    )
    spread = cumulative[:, :, None] - cumulative[:, None, :]
    decays = jnp.exp(jnp.where(linked[None], spread, -jnp.inf))
    scores = jnp.einsum("ign,jgn->gij", read_rows, write_rows, preferred_element_type=jnp.float32)
    scores = jnp.repeat(scores, repeat, axis=0)
    mixing = (decays * scores * step_size[:, None, :]).astype(jnp.bfloat16)
    within = jnp.einsum("hij,jhp->ihp", mixing, values, preferred_element_type=jnp.float32)
    inflow = jnp.exp(cumulative) * (segment_block == prior_segment)[None, :].astype(jnp.float32)
    final_segment = segment_block[-1]
    closing = (
        jnp.exp(cumulative[:, -1:] - cumulative)
        * (segment_block == final_segment)[None, :].astype(jnp.float32)
        * step_size
    )
    weighted = (values.astype(jnp.float32) * closing.T[:, :, None]).astype(jnp.bfloat16)
    writes = jnp.repeat(write_rows, repeat, axis=1)
    deposit = jnp.einsum("jhp,jhn->hpn", weighted, writes, preferred_element_type=jnp.float32)
    fading = jnp.exp(cumulative[:, -1]) * (final_segment == prior_segment).astype(jnp.float32)
    return (within, inflow, fading, deposit)


def reading(read_rows, held_state, repeat):
    readers = jnp.repeat(read_rows, repeat, axis=1).astype(jnp.float32)
    return jnp.einsum("ihn,hpn->ihp", readers, held_state, precision=highest)


def gated_norm(outputs, gates, norm_scale):
    width = INNER // GROUPS
    gated = outputs * jax.nn.silu(gates.astype(jnp.float32))
    pieces = []
    for start in range(0, outputs.shape[1], width):
        group = gated[:, start : start + width]
        mean_square = jnp.mean(group * group, axis=-1, keepdims=True)
        scaled = group * lax.rsqrt(mean_square + 1e-05) * norm_scale[start : start + width]
        pieces.append(scaled.astype(jnp.bfloat16))
    return jnp.concatenate(pieces, axis=1)


def chain_states(fading, deposit):
    half = fading.shape[0] // 2
    count = lax.axis_size("seq")
    swap = [(place, place ^ 1) for place in range(count)]
    second = lax.axis_index("seq") % 2 == 1

    def own(a):
        return jnp.where(second, a[half:], a[:half])

    def partner(a):
        return jnp.where(second, a[:half], a[half:])

    there = own(lax.ppermute(fading, "seq", swap))[:, None, None]
    here = own(fading)[:, None, None]
    other = lax.ppermute(partner(deposit).astype(jnp.bfloat16), "seq", swap).astype(jnp.float32)
    mine = own(deposit)
    early_fade, late_fade = jnp.where(second, there, here), jnp.where(second, here, there)
    early, late = jnp.where(second, other, mine), jnp.where(second, mine, other)
    added = late_fade * early + late
    scale = early_fade * late_fade
    carried = passed_along(added.astype(jnp.bfloat16), "seq", 2)
    for _ in range(-(-REACH // 2) - 1):
        held = scale * carried.astype(jnp.float32) + added
        carried = passed_along(held.astype(jnp.bfloat16), "seq", 2)
    first = carried.astype(jnp.float32)
    between = early_fade * first + early
    sent = jnp.where(second, first, between).astype(jnp.bfloat16)
    kept = jnp.where(second, between, first)
    got = lax.ppermute(sent, "seq", swap).astype(jnp.float32)
    return jnp.concatenate([jnp.where(second, got, kept), jnp.where(second, kept, got)])


def on_device(
    inner_input,
    state_input,
    gate_input,
    step_input,
    decay_exponent,
    skip_gain,
    documents,
    filter_inner,
    filter_state,
    norm_gain,
    output_weight,
):
    weight = lax.all_gather(output_weight, "seq", axis=1, tiled=True)
    margin = KERNEL - 1
    length = documents.shape[0]
    head_count = decay_exponent.shape[0]
    groups = state_input.shape[2] // STATE
    repeat = head_count // groups
    channels = inner_input.shape[1]
    state_channels = 2 * state_input.shape[2]
    halo = jnp.concatenate(
        [
            inner_input[-margin:],
            state_input[-margin:].reshape(margin, state_channels),
            jnp.broadcast_to(documents[-margin:, None].astype(jnp.bfloat16), (margin, 128)),
        ],
        axis=1,
    )
    halo = passed_along(halo, "seq", 1)
    before_inner = halo[:, :channels]
    before_state = halo[:, channels : channels + state_channels].reshape(margin, 2, -1)
    before_segments = halo[:, channels + state_channels]
    segments_wide = jnp.concatenate([before_segments.astype(jnp.int32), documents])
    inner_conv = causal_conv(
        jnp.concatenate([before_inner, inner_input]), filter_inner, segments_wide, documents
    )
    state_conv = causal_conv(
        jnp.concatenate([before_state, state_input]), filter_state, segments_wide, documents
    )
    values = inner_conv.reshape(length, head_count, HEAD_DIM)
    write_rows = state_conv[:, 0].reshape(length, groups, STATE)
    read_rows = state_conv[:, 1].reshape(length, groups, STATE)
    step_size = jax.nn.softplus(step_input)
    decay_rate = -step_size * jnp.exp(decay_exponent)[:, None]
    skipped = skip_gain[None, :, None] * values.astype(jnp.float32)
    prior_segment = segments_wide[margin - 1]
    within, inflow, fading, deposit = span_parts(
        values, write_rows, read_rows, step_size, decay_rate, documents, prior_segment
    )
    carried = chain_states(fading, deposit)
    outputs = within + inflow.T[:, :, None] * reading(read_rows, carried, repeat) + skipped
    scan_out = outputs.reshape(length, head_count * HEAD_DIM)
    normed = gated_norm(scan_out, gate_input, norm_gain)
    partial_value = jnp.dot(normed, weight, preferred_element_type=jnp.float32)
    return lax.psum_scatter(
        partial_value.astype(jnp.bfloat16), "head", scatter_dimension=1, tiled=True
    )


def solution(mesh):
    placed = (
        P("seq", "head"),
        P("seq", None, "head"),
        P("seq", "head"),
        P("head", "seq"),
        P("head"),
        P("head"),
        P("seq"),
        P(None, "head"),
        P(None, None, "head"),
        P("head"),
        P("head", "seq"),
    )
    return jax.shard_map(
        on_device, mesh=mesh, in_specs=placed, out_specs=P("seq", "head"), check_vma=False
    )
```
